32 devices in a mesh: groups: 2 (over x), vel: 16 (over z, y, core).
Axes of the slice: x: 2, y: 2, z: 4, core: 2. Of those that a mesh axis runs over, the one named last changes fastest.
Arguments:
- epoch_maps: bfloat16 [128, 192, 512], P('vel', 'groups'), parts along dimension 1, may hold values from -6 to 6, as said below
- velocity: int32 [16, 2], P('vel'), may hold values from -16 to 16, as said below
- slot_epoch: int32 [64], replicated, may hold values from 0 to 63, each once
- epoch_time: int32 [64], replicated, may hold values from 0 to 127, as said below
Outputs:
- likelihood: float32 [16, 192, 512], P('vel', 'groups'), parts along dimension 1
- best_value: float32 [192, 512], P('groups'), parts along dimension 0
The draws below stay inside these ranges and needn't reach their ends.
There are 2 independent parts, one for each index of `groups`. The reference program is written for one: setup_inputs(seed, part) draws one part's arguments, and reference() takes and returns one part's arrays. A program takes and returns all parts, laid end to end along the dimension named above; an argument that names none is the same for every part. Nothing has to cross between parts.
Inputs may be any that keep to these rules, and one draw needn't show every extreme that they name: `epoch_maps`: the first 64 images are likelihoods, the others weights of at least 0.25 and at most 4. `velocity`: all rows are distinct; rows (16, 16) and (-16, -16) both occur. `epoch_time`: strictly increasing, the first 0 and the last 127. `slot_epoch`: each epoch stands in exactly one slot.
All inputs are finite; a program needn't handle non-finite values.
Results may differ from the reference program's by a relative error of at most 0.0029.
Values may be sent and summed in bfloat16 or wider, within the bound.
A program may use at most 64 MiB of HBM per device.

```python
import jax
import jax.numpy as jnp
from jax import lax

ROWS = 96
COLS = 512
EPOCHS = 64
VMAX = 16
TMAX = 127
VELS = 16


def draw_epoch_maps(key, part):
    first_key, second_key = jax.random.split(jax.random.fold_in(key, 37), 2)
    map_shape = (EPOCHS, ROWS, COLS)
    likelihoods = jnp.clip(jax.random.normal(first_key, map_shape, jnp.float32), -6.0, 6.0)
    weights = jnp.exp(jax.random.uniform(second_key, map_shape, jnp.float32, jnp.log(0.25), jnp.log(4.0)))
    return jnp.concatenate([likelihoods, weights], axis=0).astype(jnp.bfloat16)


def draw_velocity(key, part):
    first_key, second_key = jax.random.split(jax.random.fold_in(key, 11))
    grid_side = 2 * VMAX + 1
    points = grid_side * grid_side
    shuffled = jax.random.permutation(first_key, points).astype(jnp.int32)
    extreme = (shuffled == 0) | (shuffled == points - 1)
    priority = jnp.where(extreme, (shuffled == points - 1).astype(jnp.int32) - 2, jnp.arange(points, dtype=jnp.int32))
    ranked = shuffled[jnp.argsort(priority)]
    chosen = ranked[:VELS]
    chosen = chosen[jax.random.permutation(second_key, VELS)]
    row_rate = chosen // grid_side - VMAX
    column_rate = chosen % grid_side - VMAX
    return jnp.stack([row_rate, column_rate], axis=1).astype(jnp.int32)


def draw_epoch_time(key, part):
    shuffled = jax.random.permutation(jax.random.fold_in(key, 23), TMAX + 1).astype(jnp.int32)
    extreme = (shuffled == 0) | (shuffled == TMAX)
    priority = jnp.where(extreme, (shuffled == TMAX).astype(jnp.int32) - 2, jnp.arange(TMAX + 1, dtype=jnp.int32))
    ranked = shuffled[jnp.argsort(priority)]
    return jnp.sort(ranked[:EPOCHS]).astype(jnp.int32)


def setup_inputs(seed: int = 0, part: int = 0) -> dict:
    splits = jax.random.split(jax.random.key(seed), 5)
    own_keys = jax.random.split(jax.random.fold_in(splits[4], part), 5)
    return {
        "epoch_maps": draw_epoch_maps(jax.random.fold_in(jax.random.fold_in(splits[4], part), 71), part),
        "velocity": draw_velocity(jax.random.fold_in(splits[4], 71), part),
        "slot_epoch": jax.random.permutation(splits[2], EPOCHS).astype(jnp.int32),
        "epoch_time": draw_epoch_time(jax.random.fold_in(splits[4], 71), part),
    }


SPLINE = [[64.0, 256.0, 64.0, 0.0], [27.0, 235.0, 121.0, 1.0], [8.0, 184.0, 184.0, 8.0], [1.0, 121.0, 235.0, 27.0]]
spline_norm = 147456.0
rate_divisor = 32

def spline_taps(offset):
    whole_shift = offset // 4
    fraction = offset - 4 * whole_shift
    spline_table = jnp.array(SPLINE, dtype=jnp.float32)
    return (whole_shift.astype(jnp.int32), spline_table[fraction])

def shift_axis(epoch_image, whole_shift, weights, margin, axis_number):
    widths = [(0, 0), (0, 0), (0, 0)]
    widths[axis_number] = (margin, margin)
    padded = jnp.pad(epoch_image, widths)
    length = epoch_image.shape[axis_number]
    result = jnp.zeros(epoch_image.shape, jnp.float32)
    for tap_number in range(4):
        position = (margin - 1 + tap_number + whole_shift).astype(jnp.int32)
        result = result + weights[tap_number] * lax.dynamic_slice_in_dim(padded, position, length, axis_number)
    return result

def one_epoch(epoch_image, row_offset, column_offset, margin):
    row_whole, row_weights = spline_taps(row_offset)
    rows_done = shift_axis(epoch_image.astype(jnp.float32), row_whole, row_weights, margin, 1)
    rounded = lax.optimization_barrier(rows_done.astype(jnp.bfloat16))
    column_whole, column_weights = spline_taps(column_offset)
    return shift_axis(rounded.astype(jnp.float32), column_whole, column_weights, margin, 2)

def reference(epoch_maps, velocity, slot_epoch, epoch_time):
    margin = VMAX * TMAX // 128 + 3
    images = jnp.stack([epoch_maps[:EPOCHS], epoch_maps[EPOCHS:]], axis=1)
    slot_time = epoch_time[slot_epoch]

    def per_velocity(rate_pair):
        row_offsets = rate_pair[0] * slot_time // rate_divisor
        column_offsets = rate_pair[1] * slot_time // rate_divisor
        stacks = jax.vmap(one_epoch, in_axes=(0, 0, 0, None))(images, row_offsets, column_offsets, margin)
        stack_sums = lax.optimization_barrier(jnp.sum(stacks, axis=0)) / spline_norm
        return stack_sums[0] / jnp.sqrt(stack_sums[1] + 1.0)
    likelihood = lax.map(per_velocity, velocity)
    return (likelihood, lax.optimization_barrier(jnp.max(likelihood, axis=0)))
```

```python
import functools
import math

import jax
import jax.numpy as jnp
from jax import lax
from jax.experimental import pallas as pl
from jax.experimental.pallas import tpu as pltpu
from jax.sharding import PartitionSpec as P

SPLINE = (
    (64.0, 256.0, 64.0, 0.0),
    (27.0, 235.0, 121.0, 1.0),
    (8.0, 184.0, 184.0, 8.0),
    (1.0, 121.0, 235.0, 27.0),
)
spline_norm = 147456.0
rate_divisor = 32
HALO = 64
LANES = 128


def scalar_taps(offset):
    whole = offset >> 2
    fraction = offset & 3
    taps = []
    for tap in range(4):
        value = jnp.float32(SPLINE[3][tap])
        for level in range(3):
            value = jnp.where(fraction == level, jnp.float32(SPLINE[level][tap]), value)
        taps.append(value)
    return whole, taps


def band(distance, offset):
    whole, taps = scalar_taps(offset)
    relative = distance - whole
    out = jnp.where(relative == 3, taps[3], 0.0)
    for tap in (2, 1, 0):
        out = jnp.where(relative == tap, taps[tap], out)
    return out.astype(jnp.bfloat16)


def stack_one(rate_row, rate_col, times, padded, bands, rows_done, count, rows, cols):
    blocks = cols // LANES
    row_distance = (
        lax.broadcasted_iota(jnp.int32, (rows, rows), 1)
        - lax.broadcasted_iota(jnp.int32, (rows, rows), 0)
        + 1
    )
    col_distance = (
        lax.broadcasted_iota(jnp.int32, (2 * LANES, LANES), 0)
        - lax.broadcasted_iota(jnp.int32, (2 * LANES, LANES), 1)
        + (1 - HALO)
    )
    for s in range(count):
        row_band = band(row_distance, (rate_row * times(s)) >> 5)
        bands[pl.ds(s * 2 * LANES, 2 * LANES), :] = band(
            col_distance, (rate_col * times(s)) >> 5
        )
        rows_done[s] = jnp.dot(
            row_band, padded[s], preferred_element_type=jnp.float32
        ).astype(jnp.bfloat16)
    lhs = jnp.concatenate(
        [
            jnp.concatenate(
                [rows_done[s, :, b * LANES : (b + 2) * LANES] for s in range(count)], axis=1
            )
            for b in range(blocks)
        ],
        axis=0,
    )
    return jnp.dot(lhs, bands[...], preferred_element_type=jnp.float32)


def pad_images(images, padded, count, rows, cols):
    zeros = jnp.zeros((rows, HALO), jnp.bfloat16)
    for s in range(count):
        padded[s] = jnp.concatenate([zeros, images[s], zeros], axis=1)


def stack_kernel(count, rows, cols, vel_ref, time_ref, images, out, padded, bands, rows_done):
    pad_images(images, padded, count, rows, cols)
    hypotheses = out.shape[0]

    @pl.loop(0, hypotheses)
    def _(v):
        total = stack_one(
            vel_ref[v, 0],
            vel_ref[v, 1],
            lambda s: time_ref[s],
            padded,
            bands,
            rows_done,
            count,
            rows,
            cols,
        )
        for b in range(cols // LANES):
            out[v, :, b * LANES : (b + 1) * LANES] = total[b * rows : (b + 1) * rows].astype(
                out.dtype
            )


def local(n, epoch_maps, velocity, slot_epoch, epoch_time):
    count, rows, cols = epoch_maps.shape
    epochs = slot_epoch.shape[0]
    me = lax.axis_index("vel")
    vels = lax.all_gather(velocity, "vel", axis=0, tiled=True)
    first = lax.rem(me * count, epochs)
    slots = lax.dynamic_slice_in_dim(slot_epoch, first, count, 0)
    times = epoch_time[slots]
    partial = pl.pallas_call(
        functools.partial(stack_kernel, count, rows, cols),
        out_shape=jax.ShapeDtypeStruct((vels.shape[0], rows, cols), jnp.bfloat16),
        in_specs=[
            pl.BlockSpec(memory_space=pltpu.SMEM),
            pl.BlockSpec(memory_space=pltpu.SMEM),
            pl.BlockSpec(memory_space=pltpu.VMEM),
        ],
        out_specs=pl.BlockSpec(memory_space=pltpu.VMEM),
        scratch_shapes=[
            pltpu.VMEM((count, rows, cols + 2 * HALO), jnp.bfloat16),
            pltpu.VMEM((count * 2 * LANES, LANES), jnp.bfloat16),
            pltpu.VMEM((count, rows, cols + 2 * HALO), jnp.bfloat16),
        ],
    )(vels, times, epoch_maps)
    mine = velocity.shape[0]
    received = lax.all_to_all(partial, "vel", 0, 0, tiled=True)
    received = received.reshape(2, n // 2, mine, rows, cols)
    stack_sums = jnp.sum(received.astype(jnp.float32), axis=1) / spline_norm
    likelihood = stack_sums[0] / jnp.sqrt(stack_sums[1] + 1.0)
    best_value = lax.pmax(jnp.max(likelihood, axis=0), "vel")
    return (likelihood, best_value)


def solution(mesh):
    return jax.shard_map(
        functools.partial(local, mesh.shape["vel"]),
        mesh=mesh,
        in_specs=(P("vel", "groups", None), P("vel", None), P(), P()),
        out_specs=(P("vel", "groups", None), P("groups", None)),
        check_vma=False,
    )
```

```python
import functools
import math

import jax
import jax.numpy as jnp
from jax import lax
from jax.experimental import pallas as pl
from jax.experimental.pallas import tpu as pltpu
from jax.sharding import PartitionSpec as P

SPLINE = (
    (64.0, 256.0, 64.0, 0.0),
    (27.0, 235.0, 121.0, 1.0),
    (8.0, 184.0, 184.0, 8.0),
    (1.0, 121.0, 235.0, 27.0),
)
spline_norm = 147456.0
rate_divisor = 32
HALO = 64
LANES = 128


def scalar_taps(offset):
    whole = offset >> 2
    fraction = offset & 3
    taps = []
    for tap in range(4):
        value = jnp.float32(SPLINE[3][tap])
        for level in range(3):
            value = jnp.where(fraction == level, jnp.float32(SPLINE[level][tap]), value)
        taps.append(value)
    return whole, taps


def band(distance, offset):
    whole, taps = scalar_taps(offset)
    relative = distance - whole
    out = jnp.where(relative == 3, taps[3], 0.0)
    for tap in (2, 1, 0):
        out = jnp.where(relative == tap, taps[tap], out)
    return out.astype(jnp.bfloat16)


def stack_one(rate_row, rate_col, times, padded, bands, rows_done, count, rows, cols):
    blocks = cols // LANES
    row_distance = (
        lax.broadcasted_iota(jnp.int32, (rows, rows), 1)
        - lax.broadcasted_iota(jnp.int32, (rows, rows), 0)
        + 1
    )
    col_distance = (
        lax.broadcasted_iota(jnp.int32, (2 * LANES, LANES), 0)
        - lax.broadcasted_iota(jnp.int32, (2 * LANES, LANES), 1)
        + (1 - HALO)
    )
    for s in range(count):
        row_band = band(row_distance, (rate_row * times(s)) >> 5)
        bands[pl.ds(s * 2 * LANES, 2 * LANES), :] = band(
            col_distance, (rate_col * times(s)) >> 5
        )
        rows_done[s] = jnp.dot(
            row_band, padded[s], preferred_element_type=jnp.float32
        ).astype(jnp.bfloat16)
    lhs = jnp.concatenate(
        [
            jnp.concatenate(
                [rows_done[s, :, b * LANES : (b + 2) * LANES] for s in range(count)], axis=1
            )
            for b in range(blocks)
        ],
        axis=0,
    )
    return jnp.dot(lhs, bands[...], preferred_element_type=jnp.float32)


def pad_images(images, padded, count, rows, cols):
    zeros = jnp.zeros((rows, HALO), jnp.bfloat16)
    for s in range(count):
        padded[s] = jnp.concatenate([zeros, images[s], zeros], axis=1)


def stack_kernel(count, rows, cols, vel_ref, time_ref, images, out, padded, bands, rows_done):
    pad_images(images, padded, count, rows, cols)
    hypotheses = out.shape[0]

    @pl.loop(0, hypotheses)
    def _(v):
        total = stack_one(
            vel_ref[v, 0],
            vel_ref[v, 1],
            lambda s: time_ref[s],
            padded,
            bands,
            rows_done,
            count,
            rows,
            cols,
        )
        for b in range(cols // LANES):
            out[v, :, b * LANES : (b + 1) * LANES] = total[b * rows : (b + 1) * rows].astype(
                out.dtype
            )


def fused_kernel(
    chips,
    epochs,
    count,
    rows,
    cols,
    se_ref,
    et_ref,
    vel_ref,
    images,
    like_out,
    best_out,
    peer_images,
    padded,
    bands,
    rows_done,
    vel_all,
    vel_smem,
    part_send,
    part_recv,
    like_send,
    max_send,
    max_recv,
    best_send,
    local_sem,
    image_sems,
    vel_send,
    vel_recv,
    part_ssem,
    part_rsem,
    max_sems,
    like_ssem,
    like_rsem,
    best_ssem,
    best_rsem,
):
    me = lax.axis_index("vel")
    chip, core = me // 2, me % 2
    sibling = chip * 2 + 1 - core
    blocks = cols // LANES
    slice_rows = rows * blocks // chips
    row0 = pl.multiple_of(chip // blocks * slice_rows, slice_rows)
    col0 = pl.multiple_of(chip % blocks * LANES, LANES)

    def remote(source, target, send, receive, device):
        return pltpu.make_async_remote_copy(
            src_ref=source,
            dst_ref=target,
            send_sem=send,
            recv_sem=receive,
            device_id={"vel": device},
            device_id_type=pl.DeviceIdType.MESH,
        )

    def rail(step):
        other = lax.rem(chip + step, chips)
        return other, other * 2 + core

    def each_rail(body):
        @pl.loop(1, chips)
        def _(step):
            body(*rail(step))

    barrier = pltpu.get_barrier_semaphore()
    pl.semaphore_signal(
        barrier, inc=1, device_id={"vel": sibling}, device_id_type=pl.DeviceIdType.MESH
    )
    each_rail(
        lambda other, device: pl.semaphore_signal(
            barrier, inc=1, device_id={"vel": device}, device_id_type=pl.DeviceIdType.MESH
        )
    )
    pl.semaphore_wait(barrier, chips)

    swap = remote(images, peer_images, image_sems.at[0], image_sems.at[1], sibling)
    swap.start()

    def vel_copy(other, device):
        return remote(vel_ref, vel_all.at[chip], vel_send.at[other], vel_recv.at[chip], device)

    each_rail(lambda other, device: vel_copy(other, device).start())
    own = pltpu.make_async_copy(vel_ref, vel_all.at[chip], local_sem)
    own.start()
    pad_images(images, padded, count, rows, cols)
    swap.wait_recv()
    zeros = jnp.zeros((rows, HALO), jnp.bfloat16)
    for s in range(count):
        padded[count + s] = jnp.concatenate([zeros, peer_images[s], zeros], axis=1)
    own.wait()

    def vel_arrive(other, device):
        remote(vel_ref, vel_all.at[other], vel_send.at[other], vel_recv.at[other], device).wait()

    each_rail(vel_arrive)
    to_smem = pltpu.make_async_copy(vel_all, vel_smem, local_sem)
    to_smem.start()
    to_smem.wait()

    first = lax.rem(me * count, epochs)
    peer_first = lax.rem(sibling * count, epochs)

    def time(s):
        slot = first + s if s < count else peer_first + (s - count)
        return et_ref[se_ref[slot]]

    @pl.loop(0, chips)
    def _(v):
        total = stack_one(
            vel_smem[v, 0, 0],
            vel_smem[v, 0, 1],
            time,
            padded,
            bands,
            rows_done,
            2 * count,
            rows,
            cols,
        ).astype(jnp.bfloat16)
        for t in range(chips):
            start = t % blocks * rows + t // blocks * slice_rows
            part_send[t, v] = total[start : start + slice_rows]
        part_recv[chip, v] = part_send[chip, v]
        each_rail(
            lambda other, device: remote(
                part_send.at[other, v],
                part_recv.at[chip, v],
                part_ssem.at[other],
                part_rsem.at[chip],
                device,
            ).start()
        )

    def part_arrive(other, device):
        remote(
            part_send.at[other], part_recv.at[other], part_ssem.at[other], part_rsem.at[other], device
        ).wait()

    each_rail(part_arrive)
    best = None
    for v in range(chips):
        sums = []
        for kind in range(2):
            base = kind * (chips // 2)
            acc = part_recv[base, v].astype(jnp.float32)
            for source in range(1, chips // 2):
                acc = acc + part_recv[base + source, v].astype(jnp.float32)
            sums.append(acc / spline_norm)
        value = sums[0] / jnp.sqrt(sums[1] + 1.0)
        like_send[v] = value
        best = value if best is None else jnp.maximum(best, value)
    max_send[...] = best

    meet = remote(max_send, max_recv, max_sems.at[0], max_sems.at[1], sibling)
    meet.start()

    window = (pl.ds(row0, slice_rows), pl.ds(col0, LANES))
    each_rail(
        lambda other, device: remote(
            like_send.at[other],
            like_out.at[0, window[0], window[1]],
            like_ssem.at[other],
            like_rsem.at[chip],
            device,
        ).start()
    )
    like_out[0, window[0], window[1]] = like_send[chip]
    meet.wait()
    best_send[...] = jnp.maximum(max_send[...], max_recv[...])
    each_rail(
        lambda other, device: remote(
            best_send,
            best_out.at[window[0], window[1]],
            best_ssem.at[other],
            best_rsem.at[chip],
            device,
        ).start()
    )
    best_out[window[0], window[1]] = best_send[...]

    def finish(other, device):
        theirs = (
            pl.ds(pl.multiple_of(other // blocks * slice_rows, slice_rows), slice_rows),
            pl.ds(pl.multiple_of(other % blocks * LANES, LANES), LANES),
        )
        remote(
            like_send.at[other],
            like_out.at[0, theirs[0], theirs[1]],
            like_ssem.at[other],
            like_rsem.at[other],
            device,
        ).wait()
        remote(
            best_send,
            best_out.at[theirs[0], theirs[1]],
            best_ssem.at[other],
            best_rsem.at[other],
            device,
        ).wait()

    each_rail(finish)
    swap.wait_send()


def fused(n, epoch_maps, velocity, slot_epoch, epoch_time):
    count, rows, cols = epoch_maps.shape
    epochs = slot_epoch.shape[0]
    chips = n // 2
    slice_rows = rows * (cols // LANES) // chips
    vel_tile = jnp.broadcast_to(jnp.pad(velocity, ((0, 0), (0, LANES - 2))), (8, LANES))
    smem = pl.BlockSpec(memory_space=pltpu.SMEM)
    vmem = pl.BlockSpec(memory_space=pltpu.VMEM)
    f32, bf16 = jnp.float32, jnp.bfloat16
    dma = pltpu.SemaphoreType.DMA
    return pl.pallas_call(
        functools.partial(fused_kernel, chips, epochs, count, rows, cols),
        out_shape=(
            jax.ShapeDtypeStruct((1, rows, cols), f32),
            jax.ShapeDtypeStruct((rows, cols), f32),
        ),
        in_specs=[smem, smem, vmem, vmem],
        out_specs=(vmem, vmem),
        scratch_shapes=[
            pltpu.VMEM((count, rows, cols), bf16),
            pltpu.VMEM((2 * count, rows, cols + 2 * HALO), bf16),
            pltpu.VMEM((2 * count * 2 * LANES, LANES), bf16),
            pltpu.VMEM((2 * count, rows, cols + 2 * HALO), bf16),
            pltpu.VMEM((chips, 8, LANES), jnp.int32),
            pltpu.SMEM((chips, 8, LANES), jnp.int32),
            pltpu.VMEM((chips, chips, slice_rows, LANES), bf16),
            pltpu.VMEM((chips, chips, slice_rows, LANES), bf16),
            pltpu.VMEM((chips, slice_rows, LANES), f32),
            pltpu.VMEM((slice_rows, LANES), f32),
            pltpu.VMEM((slice_rows, LANES), f32),
            pltpu.VMEM((slice_rows, LANES), f32),
            dma,
            dma((2,)),
            dma((chips,)),
            dma((chips,)),
            dma((chips,)),
            dma((chips,)),
            dma((2,)),
            dma((chips,)),
            dma((chips,)),
            dma((chips,)),
            dma((chips,)),
        ],
        compiler_params=pltpu.CompilerParams(collective_id=0, has_side_effects=True),
    )(slot_epoch, epoch_time, vel_tile, epoch_maps)


def fits(n, epoch_maps, velocity, epochs):
    count, rows, cols = epoch_maps.shape
    chips = n // 2
    blocks = cols // LANES
    return (
        n % 4 == 0
        and velocity.shape[0] == 1
        and n * count == 2 * epochs
        and cols % LANES == 0
        and chips % blocks == 0
        and rows % (chips // blocks * 16) == 0
    )


def local(n, epoch_maps, velocity, slot_epoch, epoch_time):
    count, rows, cols = epoch_maps.shape
    epochs = slot_epoch.shape[0]
    if fits(n, epoch_maps, velocity, epochs):
        return fused(n, epoch_maps, velocity, slot_epoch, epoch_time)
    me = lax.axis_index("vel")
    vels = lax.all_gather(velocity, "vel", axis=0, tiled=True)
    first = lax.rem(me * count, epochs)
    slots = lax.dynamic_slice_in_dim(slot_epoch, first, count, 0)
    times = epoch_time[slots]
    partial = pl.pallas_call(
        functools.partial(stack_kernel, count, rows, cols),
        out_shape=jax.ShapeDtypeStruct((vels.shape[0], rows, cols), jnp.bfloat16),
        in_specs=[
            pl.BlockSpec(memory_space=pltpu.SMEM),
            pl.BlockSpec(memory_space=pltpu.SMEM),
            pl.BlockSpec(memory_space=pltpu.VMEM),
        ],
        out_specs=pl.BlockSpec(memory_space=pltpu.VMEM),
        scratch_shapes=[
            pltpu.VMEM((count, rows, cols + 2 * HALO), jnp.bfloat16),
            pltpu.VMEM((count * 2 * LANES, LANES), jnp.bfloat16),
            pltpu.VMEM((count, rows, cols + 2 * HALO), jnp.bfloat16),
        ],
    )(vels, times, epoch_maps)
    mine = velocity.shape[0]
    received = lax.all_to_all(partial, "vel", 0, 0, tiled=True)
    received = received.reshape(2, n // 2, mine, rows, cols)
    stack_sums = jnp.sum(received.astype(jnp.float32), axis=1) / spline_norm
    likelihood = stack_sums[0] / jnp.sqrt(stack_sums[1] + 1.0)
    best_value = lax.pmax(jnp.max(likelihood, axis=0), "vel")
    return (likelihood, best_value)


def solution(mesh):
    return jax.shard_map(
        functools.partial(local, mesh.shape["vel"]),
        mesh=mesh,
        in_specs=(P("vel", "groups", None), P("vel", None), P(), P()),
        out_specs=(P("vel", "groups", None), P("groups", None)),
        check_vma=False,
    )
```

```python
import functools
import math

import jax
import jax.numpy as jnp
from jax import lax
from jax.experimental import pallas as pl
from jax.experimental.pallas import tpu as pltpu
from jax.sharding import PartitionSpec as P

SPLINE = (
    (64.0, 256.0, 64.0, 0.0),
    (27.0, 235.0, 121.0, 1.0),
    (8.0, 184.0, 184.0, 8.0),
    (1.0, 121.0, 235.0, 27.0),
)
spline_norm = 147456.0
rate_divisor = 32
HALO = 64
LANES = 128


def scalar_taps(offset):
    whole = offset >> 2
    fraction = offset & 3
    taps = []
    for tap in range(4):
        value = jnp.float32(SPLINE[3][tap])
        for level in range(3):
            value = jnp.where(fraction == level, jnp.float32(SPLINE[level][tap]), value)
        taps.append(value)
    return whole, taps


def band(distance, offset):
    whole, taps = scalar_taps(offset)
    relative = distance - whole
    out = jnp.where(relative == 3, taps[3], 0.0)
    for tap in (2, 1, 0):
        out = jnp.where(relative == tap, taps[tap], out)
    return out.astype(jnp.bfloat16)


def stack_one(rate_row, rate_col, times, padded, bands, rows_done, count, rows, cols):
    blocks = cols // LANES
    row_distance = (
        lax.broadcasted_iota(jnp.int32, (rows, rows), 1)
        - lax.broadcasted_iota(jnp.int32, (rows, rows), 0)
        + 1
    )
    col_distance = (
        lax.broadcasted_iota(jnp.int32, (2 * LANES, LANES), 0)
        - lax.broadcasted_iota(jnp.int32, (2 * LANES, LANES), 1)
        + (1 - HALO)
    )
    for s in range(count):
        row_band = band(row_distance, (rate_row * times(s)) >> 5)
        bands[pl.ds(s * 2 * LANES, 2 * LANES), :] = band(
            col_distance, (rate_col * times(s)) >> 5
        )
        rows_done[s] = jnp.dot(
            row_band, padded[s], preferred_element_type=jnp.float32
        ).astype(jnp.bfloat16)
    lhs = jnp.concatenate(
        [
            jnp.concatenate(
                [rows_done[s, :, b * LANES : (b + 2) * LANES] for s in range(count)], axis=1
            )
            for b in range(blocks)
        ],
        axis=0,
    )
    return jnp.dot(lhs, bands[...], preferred_element_type=jnp.float32)


def pad_images(images, padded, start, count):
    zeros = jnp.zeros((images.shape[1], HALO), jnp.bfloat16)
    for s in range(count):
        padded[start + s] = jnp.concatenate([zeros, images[s], zeros], axis=1)


def stack_kernel(count, rows, cols, vel_ref, time_ref, images, out, padded, bands, rows_done):
    pad_images(images, padded, 0, count)
    hypotheses = out.shape[0]

    @pl.loop(0, hypotheses)
    def _(v):
        total = stack_one(
            vel_ref[v, 0],
            vel_ref[v, 1],
            lambda s: time_ref[s],
            padded,
            bands,
            rows_done,
            count,
            rows,
            cols,
        )
        for b in range(cols // LANES):
            out[v, :, b * LANES : (b + 1) * LANES] = total[b * rows : (b + 1) * rows].astype(
                out.dtype
            )


def fused_kernel(
    chips,
    epochs,
    count,
    rows,
    cols,
    se_ref,
    et_ref,
    vel_ref,
    images,
    like_out,
    best_out,
    peer_images,
    padded,
    bands,
    rows_done,
    vel_all,
    part_send,
    part_recv,
    far_own,
    hop_recv,
    far_send,
    like_send,
    max_send,
    max_recv,
    best_send,
    image_sems,
    vel_send,
    vel_recv,
    part_ssem,
    part_rsem,
    hop_ssem,
    hop_rsem,
    max_sems,
    like_ssem,
    like_rsem,
    best_ssem,
    best_rsem,
):
    me = lax.axis_index("vel")
    chip, core = me // 2, me % 2
    sibling = chip * 2 + 1 - core
    blocks = cols // LANES
    half, quarter = chips // 2, chips // 4
    slice_rows = rows * blocks // chips
    near0 = chip // half * half
    far0 = half - near0
    group = chip // quarter
    inner = (group + 1) // 2 % 2
    partner = chip + quarter * (1 - 2 * (group % 2))
    far_inner = quarter * (2 - chip // half)

    def window(owner):
        return (
            pl.ds(pl.multiple_of(owner // blocks * slice_rows, slice_rows), slice_rows),
            pl.ds(pl.multiple_of(owner % blocks * LANES, LANES), LANES),
        )

    def remote(source, target, send, receive, device):
        return pltpu.make_async_remote_copy(
            src_ref=source,
            dst_ref=target,
            send_sem=send,
            recv_sem=receive,
            device_id={"vel": device},
            device_id_type=pl.DeviceIdType.MESH,
        )

    def rail(other):
        return other * 2 + core

    def each_rail(body):
        @pl.loop(1, chips)
        def _(step):
            body(lax.rem(chip + step, chips))

    def each_near(body):
        @pl.loop(1, half)
        def _(step):
            body(near0 + lax.rem(chip - near0 + step, half))

    def greet(device):
        pl.semaphore_signal(
            barrier, inc=1, device_id={"vel": device}, device_id_type=pl.DeviceIdType.MESH
        )

    barrier = pltpu.get_barrier_semaphore()
    greet(sibling)
    each_rail(lambda other: greet(rail(other)))
    pad_images(images, padded, 0, count)
    max_send[...] = jnp.full_like(max_send, -jnp.inf)
    pl.semaphore_wait(barrier, chips)

    def vel_copy(source, target, other):
        return remote(vel_ref, vel_all.at[target], vel_send.at[source], vel_recv.at[target], rail(other))

    each_rail(lambda other: vel_copy(other, chip, other).start())
    swap = remote(images, peer_images, image_sems.at[0], image_sems.at[1], sibling)
    swap.start()
    vel_all[chip, 0, 0] = vel_ref[0, 0]
    vel_all[chip, 0, 1] = vel_ref[0, 1]
    swap.wait_recv()
    pad_images(peer_images, padded, count, count)
    each_rail(lambda other: vel_copy(other, other, other).wait())

    first = lax.rem(me * count, epochs)
    peer_first = lax.rem(sibling * count, epochs)

    def time(s):
        slot = first + s if s < count else peer_first + (s - count)
        return et_ref[se_ref[slot]]

    def part_copy(v, source, other):
        return remote(
            part_send.at[v, other],
            part_recv.at[v, source],
            part_ssem.at[v, other],
            part_rsem.at[v, source],
            rail(other),
        )

    def far_copy(v, step, source):
        other = far0 + step
        return remote(
            far_send.at[v, step],
            part_recv.at[v, source],
            part_ssem.at[v, other],
            part_rsem.at[v, source],
            rail(other),
        )

    def hop_copy(v):
        return remote(
            part_send.at[v, pl.ds(far0, half)],
            hop_recv.at[v],
            hop_ssem.at[v],
            hop_rsem.at[v],
            rail(partner),
        )

    def like_copy(v, owner):
        return remote(
            like_send.at[v],
            like_out.at[0, window(owner)[0], window(owner)[1]],
            like_ssem.at[v],
            like_rsem.at[owner],
            rail(v),
        )

    def forward(v):
        @pl.when(inner == 1)
        def _():
            hop_copy(v).wait_recv()

            @pl.loop(0, half)
            def _(step):
                total = far_own[v % 2, far0 + step] + hop_recv[v, step].astype(jnp.float32)
                far_send[v, step] = total.astype(jnp.bfloat16)
                far_copy(v, step, chip).start()

    def finish_like(v):
        each_near(lambda other: part_copy(v, other, other).wait_recv())

        @pl.loop(0, quarter)
        def _(step):
            far_copy(v, 0, far_inner + step).wait_recv()

        near = part_recv[v, near0].astype(jnp.float32)
        for step in range(1, half):
            near = near + part_recv[v, near0 + step].astype(jnp.float32)
        far = part_recv[v, far_inner].astype(jnp.float32)
        for step in range(1, quarter):
            far = far + part_recv[v, far_inner + step].astype(jnp.float32)
        first_kind = near0 == 0
        signal = jnp.where(first_kind, near, far) / spline_norm
        weight = jnp.where(first_kind, far, near) / spline_norm
        value = signal / jnp.sqrt(weight + 1.0)
        max_send[...] = jnp.maximum(max_send[...], value)
        like_send[v] = value

        @pl.when(v != chip)
        def _():
            like_copy(v, chip).start()

    late = 3

    @pl.loop(0, chips)
    def _(v):
        total = stack_one(
            vel_all[v, 0, 0],
            vel_all[v, 0, 1],
            time,
            padded,
            bands,
            rows_done,
            2 * count,
            rows,
            cols,
        )
        for t in range(chips):
            start = t % blocks * rows + t // blocks * slice_rows
            piece = total[start : start + slice_rows]
            far_own[v % 2, t] = piece
            part_send[v, t] = piece.astype(jnp.bfloat16)
        part_recv[v, chip] = part_send[v, chip]

        @pl.when(inner == 0)
        def _():
            hop_copy(v).start()

        each_near(lambda other: part_copy(v, chip, other).start())

        @pl.when(v >= 1)
        def _():
            forward(v - 1)

        @pl.when(v >= late)
        def _():
            finish_like(v - late)

    forward(chips - 1)

    @pl.loop(chips - late, chips)
    def _(v):
        finish_like(v)

    meet = remote(max_send, max_recv, max_sems.at[0], max_sems.at[1], sibling)
    meet.start()
    like_out[0, window(chip)[0], window(chip)[1]] = like_send[chip]
    meet.wait()
    best_send[...] = jnp.maximum(max_send[...], max_recv[...])

    def best_copy(owner, other):
        return remote(
            best_send,
            best_out.at[window(owner)[0], window(owner)[1]],
            best_ssem.at[other],
            best_rsem.at[owner],
            rail(other),
        )

    each_rail(lambda other: best_copy(chip, other).start())
    best_out[window(chip)[0], window(chip)[1]] = best_send[...]

    @pl.loop(0, chips)
    def _(v):
        each_near(lambda other: part_copy(v, chip, other).wait_send())

        @pl.when(inner == 0)
        def _():
            hop_copy(v).wait_send()

        @pl.when(inner == 1)
        def _():
            @pl.loop(0, half)
            def _(step):
                far_copy(v, step, chip).wait_send()

    swap.wait_send()

    def finish(other):
        like_copy(other, other).wait()
        best_copy(other, other).wait()

    each_rail(finish)


def fused(n, epoch_maps, velocity, slot_epoch, epoch_time):
    count, rows, cols = epoch_maps.shape
    epochs = slot_epoch.shape[0]
    chips = n // 2
    half = chips // 2
    slice_rows = rows * (cols // LANES) // chips
    smem = pl.BlockSpec(memory_space=pltpu.SMEM)
    vmem = pl.BlockSpec(memory_space=pltpu.VMEM)
    f32, bf16 = jnp.float32, jnp.bfloat16
    dma = pltpu.SemaphoreType.DMA
    return pl.pallas_call(
        functools.partial(fused_kernel, chips, epochs, count, rows, cols),
        out_shape=(
            jax.ShapeDtypeStruct((1, rows, cols), f32),
            jax.ShapeDtypeStruct((rows, cols), f32),
        ),
        in_specs=[smem, smem, smem, vmem],
        out_specs=(vmem, vmem),
        scratch_shapes=[
            pltpu.VMEM((count, rows, cols), bf16),
            pltpu.VMEM((2 * count, rows, cols + 2 * HALO), bf16),
            pltpu.VMEM((2 * count * 2 * LANES, LANES), bf16),
            pltpu.VMEM((2 * count, rows, cols + 2 * HALO), bf16),
            pltpu.SMEM((chips, 1, 2), jnp.int32),
            pltpu.VMEM((chips, chips, slice_rows, LANES), bf16),
            pltpu.VMEM((chips, chips, slice_rows, LANES), bf16),
            pltpu.VMEM((2, chips, slice_rows, LANES), f32),
            pltpu.VMEM((chips, half, slice_rows, LANES), bf16),
            pltpu.VMEM((chips, half, slice_rows, LANES), bf16),
            pltpu.VMEM((chips, slice_rows, LANES), f32),
            pltpu.VMEM((slice_rows, LANES), f32),
            pltpu.VMEM((slice_rows, LANES), f32),
            pltpu.VMEM((slice_rows, LANES), f32),
            dma((2,)),
            dma((chips,)),
            dma((chips,)),
            dma((chips, chips)),
            dma((chips, chips)),
            dma((chips,)),
            dma((chips,)),
            dma((2,)),
            dma((chips,)),
            dma((chips,)),
            dma((chips,)),
            dma((chips,)),
        ],
        compiler_params=pltpu.CompilerParams(collective_id=0, has_side_effects=True),
    )(slot_epoch, epoch_time, velocity, epoch_maps)


def fits(n, epoch_maps, velocity, epochs):
    count, rows, cols = epoch_maps.shape
    chips = n // 2
    blocks = cols // LANES
    return (
        n % 4 == 0
        and velocity.shape[0] == 1
        and n * count == 2 * epochs
        and cols % LANES == 0
        and chips % blocks == 0
        and rows % (chips // blocks * 16) == 0
    )


def local(n, epoch_maps, velocity, slot_epoch, epoch_time):
    count, rows, cols = epoch_maps.shape
    epochs = slot_epoch.shape[0]
    if fits(n, epoch_maps, velocity, epochs):
        return fused(n, epoch_maps, velocity, slot_epoch, epoch_time)
    me = lax.axis_index("vel")
    vels = lax.all_gather(velocity, "vel", axis=0, tiled=True)
    first = lax.rem(me * count, epochs)
    slots = lax.dynamic_slice_in_dim(slot_epoch, first, count, 0)
    times = epoch_time[slots]
    partial = pl.pallas_call(
        functools.partial(stack_kernel, count, rows, cols),
        out_shape=jax.ShapeDtypeStruct((vels.shape[0], rows, cols), jnp.bfloat16),
        in_specs=[
            pl.BlockSpec(memory_space=pltpu.SMEM),
            pl.BlockSpec(memory_space=pltpu.SMEM),
            pl.BlockSpec(memory_space=pltpu.VMEM),
        ],
        out_specs=pl.BlockSpec(memory_space=pltpu.VMEM),
        scratch_shapes=[
            pltpu.VMEM((count, rows, cols + 2 * HALO), jnp.bfloat16),
            pltpu.VMEM((count * 2 * LANES, LANES), jnp.bfloat16),
            pltpu.VMEM((count, rows, cols + 2 * HALO), jnp.bfloat16),
        ],
    )(vels, times, epoch_maps)
    mine = velocity.shape[0]
    received = lax.all_to_all(partial, "vel", 0, 0, tiled=True)
    received = received.reshape(2, n // 2, mine, rows, cols)
    stack_sums = jnp.sum(received.astype(jnp.float32), axis=1) / spline_norm
    likelihood = stack_sums[0] / jnp.sqrt(stack_sums[1] + 1.0)
    best_value = lax.pmax(jnp.max(likelihood, axis=0), "vel")
    return (likelihood, best_value)


def solution(mesh):
    return jax.shard_map(
        functools.partial(local, mesh.shape["vel"]),
        mesh=mesh,
        in_specs=(P("vel", "groups", None), P("vel", None), P(), P()),
        out_specs=(P("vel", "groups", None), P("groups", None)),
        check_vma=False,
    )
```

```python
import functools
import math

import jax
import jax.numpy as jnp
from jax import lax
from jax.experimental import pallas as pl
from jax.experimental.pallas import tpu as pltpu
from jax.sharding import PartitionSpec as P

SPLINE = (
    (64.0, 256.0, 64.0, 0.0),
    (27.0, 235.0, 121.0, 1.0),
    (8.0, 184.0, 184.0, 8.0),
    (1.0, 121.0, 235.0, 27.0),
)
spline_norm = 147456.0
rate_divisor = 32
HALO = 64
LANES = 128


def scalar_taps(offset):
    whole = offset >> 2
    fraction = offset & 3
    taps = []
    for tap in range(4):
        value = jnp.float32(SPLINE[3][tap])
        for level in range(3):
            value = jnp.where(fraction == level, jnp.float32(SPLINE[level][tap]), value)
        taps.append(value)
    return whole, taps


def band(distance, offset):
    whole, taps = scalar_taps(offset)
    relative = distance - whole
    out = jnp.where(relative == 3, taps[3], 0.0)
    for tap in (2, 1, 0):
        out = jnp.where(relative == tap, taps[tap], out)
    return out.astype(jnp.bfloat16)


def stack_one(rate_row, rate_col, times, padded, bands, rows_done, count, rows, cols):
    blocks = cols // LANES
    row_distance = (
        lax.broadcasted_iota(jnp.int32, (rows, rows), 1)
        - lax.broadcasted_iota(jnp.int32, (rows, rows), 0)
        + 1
    )
    col_distance = (
        lax.broadcasted_iota(jnp.int32, (2 * LANES, LANES), 0)
        - lax.broadcasted_iota(jnp.int32, (2 * LANES, LANES), 1)
        + (1 - HALO)
    )
    for s in range(count):
        row_band = band(row_distance, (rate_row * times(s)) >> 5)
        bands[pl.ds(s * 2 * LANES, 2 * LANES), :] = band(
            col_distance, (rate_col * times(s)) >> 5
        )
        rows_done[s] = jnp.dot(
            row_band, padded[s], preferred_element_type=jnp.float32
        ).astype(jnp.bfloat16)
    lhs = jnp.concatenate(
        [
            jnp.concatenate(
                [rows_done[s, :, b * LANES : (b + 2) * LANES] for s in range(count)], axis=1
            )
            for b in range(blocks)
        ],
        axis=0,
    )
    return jnp.dot(lhs, bands[...], preferred_element_type=jnp.float32)


def pad_images(images, padded, start, count):
    zeros = jnp.zeros((images.shape[1], HALO), jnp.bfloat16)
    for s in range(count):
        padded[start + s] = jnp.concatenate([zeros, images[s], zeros], axis=1)


def stack_kernel(count, rows, cols, vel_ref, time_ref, images, out, padded, bands, rows_done):
    pad_images(images, padded, 0, count)
    hypotheses = out.shape[0]

    @pl.loop(0, hypotheses)
    def _(v):
        total = stack_one(
            vel_ref[v, 0],
            vel_ref[v, 1],
            lambda s: time_ref[s],
            padded,
            bands,
            rows_done,
            count,
            rows,
            cols,
        )
        for b in range(cols // LANES):
            out[v, :, b * LANES : (b + 1) * LANES] = total[b * rows : (b + 1) * rows].astype(
                out.dtype
            )


def fused_kernel(
    chips,
    epochs,
    count,
    rows,
    cols,
    se_ref,
    et_ref,
    vel_ref,
    images,
    out_ref,
    peer_images,
    padded,
    bands,
    rows_done,
    vel_all,
    part_send,
    part_recv,
    far_own,
    hop_recv,
    far_send,
    like_send,
    max_send,
    max_recv,
    best_send,
    image_sems,
    vel_send,
    vel_recv,
    part_ssem,
    part_rsem,
    hop_ssem,
    hop_rsem,
    max_sems,
    like_ssem,
    like_rsem,
    best_ssem,
    best_rsem,
):
    like_out, best_out = out_ref.at[pl.ds(0, 1)], out_ref.at[1]
    me = lax.axis_index("vel")
    chip, core = me // 2, me % 2
    sibling = chip * 2 + 1 - core
    blocks = cols // LANES
    half, quarter = chips // 2, chips // 4
    slice_rows = rows * blocks // chips
    near0 = chip // half * half
    far0 = half - near0
    group = chip // quarter
    inner = (group + 1) // 2 % 2
    partner = chip + quarter * (1 - 2 * (group % 2))
    far_inner = quarter * (2 - chip // half)

    def window(owner):
        return (
            pl.ds(pl.multiple_of(owner // blocks * slice_rows, slice_rows), slice_rows),
            pl.ds(pl.multiple_of(owner % blocks * LANES, LANES), LANES),
        )

    def remote(source, target, send, receive, device):
        return pltpu.make_async_remote_copy(
            src_ref=source,
            dst_ref=target,
            send_sem=send,
            recv_sem=receive,
            device_id={"vel": device},
            device_id_type=pl.DeviceIdType.MESH,
        )

    def rail(other):
        return other * 2 + core

    def each_rail(body):
        @pl.loop(1, chips)
        def _(step):
            body(lax.rem(chip + step, chips))

    def each_near(body):
        @pl.loop(1, half)
        def _(step):
            body(near0 + lax.rem(chip - near0 + step, half))

    def greet(device):
        pl.semaphore_signal(
            barrier, inc=1, device_id={"vel": device}, device_id_type=pl.DeviceIdType.MESH
        )

    barrier = pltpu.get_barrier_semaphore()
    greet(sibling)
    each_rail(lambda other: greet(rail(other)))
    pad_images(images, padded, 0, count)
    max_send[...] = jnp.full_like(max_send, -jnp.inf)
    pl.semaphore_wait(barrier, chips)

    def vel_copy(source, target, other):
        return remote(vel_ref, vel_all.at[target], vel_send.at[source], vel_recv.at[target], rail(other))

    each_rail(lambda other: vel_copy(other, chip, other).start())
    swap = remote(images, peer_images, image_sems.at[0], image_sems.at[1], sibling)
    swap.start()
    vel_all[chip, 0, 0] = vel_ref[0, 0]
    vel_all[chip, 0, 1] = vel_ref[0, 1]
    swap.wait_recv()
    pad_images(peer_images, padded, count, count)
    each_rail(lambda other: vel_copy(other, other, other).wait())

    first = lax.rem(me * count, epochs)
    peer_first = lax.rem(sibling * count, epochs)

    def time(s):
        slot = first + s if s < count else peer_first + (s - count)
        return et_ref[se_ref[slot]]

    def part_copy(v, source, other):
        return remote(
            part_send.at[v, other],
            part_recv.at[v, source],
            part_ssem.at[v, other],
            part_rsem.at[v, source],
            rail(other),
        )

    def far_copy(v, step, source):
        other = far0 + step
        return remote(
            far_send.at[v, step],
            part_recv.at[v, source],
            part_ssem.at[v, other],
            part_rsem.at[v, source],
            rail(other),
        )

    def hop_copy(v):
        return remote(
            part_send.at[v, pl.ds(far0, half)],
            hop_recv.at[v],
            hop_ssem.at[v],
            hop_rsem.at[v],
            rail(partner),
        )

    def like_copy(v, owner):
        return remote(
            like_send.at[v],
            like_out.at[0, window(owner)[0], window(owner)[1]],
            like_ssem.at[v],
            like_rsem.at[owner],
            rail(v),
        )

    def forward(v):
        @pl.when(inner == 1)
        def _():
            hop_copy(v).wait_recv()

            @pl.loop(0, half)
            def _(step):
                total = far_own[v % 2, far0 + step] + hop_recv[v, step].astype(jnp.float32)
                far_send[v, step] = total.astype(jnp.bfloat16)
                far_copy(v, step, chip).start()

    def finish_like(v):
        each_near(lambda other: part_copy(v, other, other).wait_recv())

        @pl.loop(0, quarter)
        def _(step):
            far_copy(v, 0, far_inner + step).wait_recv()

        near = part_recv[v, near0].astype(jnp.float32)
        for step in range(1, half):
            near = near + part_recv[v, near0 + step].astype(jnp.float32)
        far = part_recv[v, far_inner].astype(jnp.float32)
        for step in range(1, quarter):
            far = far + part_recv[v, far_inner + step].astype(jnp.float32)
        first_kind = near0 == 0
        signal = jnp.where(first_kind, near, far) / spline_norm
        weight = jnp.where(first_kind, far, near) / spline_norm
        value = signal / jnp.sqrt(weight + 1.0)
        max_send[...] = jnp.maximum(max_send[...], value)
        like_send[v] = value

        @pl.when(v != chip)
        def _():
            like_copy(v, chip).start()

    late = 3

    @pl.loop(0, chips)
    def _(v):
        total = stack_one(
            vel_all[v, 0, 0],
            vel_all[v, 0, 1],
            time,
            padded,
            bands,
            rows_done,
            2 * count,
            rows,
            cols,
        )
        for t in range(chips):
            start = t % blocks * rows + t // blocks * slice_rows
            piece = total[start : start + slice_rows]
            far_own[v % 2, t] = piece
            part_send[v, t] = piece.astype(jnp.bfloat16)
        part_recv[v, chip] = part_send[v, chip]

        @pl.when(inner == 0)
        def _():
            hop_copy(v).start()

        each_near(lambda other: part_copy(v, chip, other).start())

        @pl.when(v >= 1)
        def _():
            forward(v - 1)

        @pl.when(v >= late)
        def _():
            finish_like(v - late)

    forward(chips - 1)

    @pl.loop(chips - late, chips)
    def _(v):
        finish_like(v)

    meet = remote(max_send, max_recv, max_sems.at[0], max_sems.at[1], sibling)
    meet.start()
    like_out[0, window(chip)[0], window(chip)[1]] = like_send[chip]
    meet.wait()
    best_send[...] = jnp.maximum(max_send[...], max_recv[...])

    def best_copy(owner, other):
        return remote(
            best_send,
            best_out.at[window(owner)[0], window(owner)[1]],
            best_ssem.at[other],
            best_rsem.at[owner],
            rail(other),
        )

    each_rail(lambda other: best_copy(chip, other).start())
    best_out[window(chip)[0], window(chip)[1]] = best_send[...]

    @pl.loop(0, chips)
    def _(v):
        each_near(lambda other: part_copy(v, chip, other).wait_send())

        @pl.when(inner == 0)
        def _():
            hop_copy(v).wait_send()

        @pl.when(inner == 1)
        def _():
            @pl.loop(0, half)
            def _(step):
                far_copy(v, step, chip).wait_send()

    swap.wait_send()

    def finish(other):
        like_copy(other, other).wait()
        best_copy(other, other).wait()

    each_rail(finish)


def fused(n, epoch_maps, velocity, slot_epoch, epoch_time):
    count, rows, cols = epoch_maps.shape
    epochs = slot_epoch.shape[0]
    chips = n // 2
    half = chips // 2
    slice_rows = rows * (cols // LANES) // chips
    smem = pl.BlockSpec(memory_space=pltpu.SMEM)
    vmem = pl.BlockSpec(memory_space=pltpu.VMEM)
    f32, bf16 = jnp.float32, jnp.bfloat16
    dma = pltpu.SemaphoreType.DMA
    both = pl.pallas_call(
        functools.partial(fused_kernel, chips, epochs, count, rows, cols),
        out_shape=jax.ShapeDtypeStruct((2, rows, cols), f32),
        in_specs=[smem, smem, smem, vmem],
        out_specs=vmem,
        scratch_shapes=[
            pltpu.VMEM((count, rows, cols), bf16),
            pltpu.VMEM((2 * count, rows, cols + 2 * HALO), bf16),
            pltpu.VMEM((2 * count * 2 * LANES, LANES), bf16),
            pltpu.VMEM((2 * count, rows, cols + 2 * HALO), bf16),
            pltpu.SMEM((chips, 1, 2), jnp.int32),
            pltpu.VMEM((chips, chips, slice_rows, LANES), bf16),
            pltpu.VMEM((chips, chips, slice_rows, LANES), bf16),
            pltpu.VMEM((2, chips, slice_rows, LANES), f32),
            pltpu.VMEM((chips, half, slice_rows, LANES), bf16),
            pltpu.VMEM((chips, half, slice_rows, LANES), bf16),
            pltpu.VMEM((chips, slice_rows, LANES), f32),
            pltpu.VMEM((slice_rows, LANES), f32),
            pltpu.VMEM((slice_rows, LANES), f32),
            pltpu.VMEM((slice_rows, LANES), f32),
            dma((2,)),
            dma((chips,)),
            dma((chips,)),
            dma((chips, chips)),
            dma((chips, chips)),
            dma((chips,)),
            dma((chips,)),
            dma((2,)),
            dma((chips,)),
            dma((chips,)),
            dma((chips,)),
            dma((chips,)),
        ],
        compiler_params=pltpu.CompilerParams(collective_id=0, has_side_effects=True),
    )(slot_epoch, epoch_time, velocity, epoch_maps)
    return (both[:1], both[1])


def fits(n, epoch_maps, velocity, epochs):
    count, rows, cols = epoch_maps.shape
    chips = n // 2
    blocks = cols // LANES
    return (
        n % 4 == 0
        and velocity.shape[0] == 1
        and n * count == 2 * epochs
        and cols % LANES == 0
        and chips % blocks == 0
        and rows % (chips // blocks * 16) == 0
    )


def local(n, epoch_maps, velocity, slot_epoch, epoch_time):
    count, rows, cols = epoch_maps.shape
    epochs = slot_epoch.shape[0]
    if fits(n, epoch_maps, velocity, epochs):
        return fused(n, epoch_maps, velocity, slot_epoch, epoch_time)
    me = lax.axis_index("vel")
    vels = lax.all_gather(velocity, "vel", axis=0, tiled=True)
    first = lax.rem(me * count, epochs)
    slots = lax.dynamic_slice_in_dim(slot_epoch, first, count, 0)
    times = epoch_time[slots]
    partial = pl.pallas_call(
        functools.partial(stack_kernel, count, rows, cols),
        out_shape=jax.ShapeDtypeStruct((vels.shape[0], rows, cols), jnp.bfloat16),
        in_specs=[
            pl.BlockSpec(memory_space=pltpu.SMEM),
            pl.BlockSpec(memory_space=pltpu.SMEM),
            pl.BlockSpec(memory_space=pltpu.VMEM),
        ],
        out_specs=pl.BlockSpec(memory_space=pltpu.VMEM),
        scratch_shapes=[
            pltpu.VMEM((count, rows, cols + 2 * HALO), jnp.bfloat16),
            pltpu.VMEM((count * 2 * LANES, LANES), jnp.bfloat16),
            pltpu.VMEM((count, rows, cols + 2 * HALO), jnp.bfloat16),
        ],
    )(vels, times, epoch_maps)
    mine = velocity.shape[0]
    received = lax.all_to_all(partial, "vel", 0, 0, tiled=True)
    received = received.reshape(2, n // 2, mine, rows, cols)
    stack_sums = jnp.sum(received.astype(jnp.float32), axis=1) / spline_norm
    likelihood = stack_sums[0] / jnp.sqrt(stack_sums[1] + 1.0)
    best_value = lax.pmax(jnp.max(likelihood, axis=0), "vel")
    return (likelihood, best_value)


def solution(mesh):
    return jax.shard_map(
        functools.partial(local, mesh.shape["vel"]),
        mesh=mesh,
        in_specs=(P("vel", "groups", None), P("vel", None), P(), P()),
        out_specs=(P("vel", "groups", None), P("groups", None)),
        check_vma=False,
    )
```
